32 devices in a mesh: row: 4 (over z), col: 8 (over y, x, core).
Axes of the slice: x: 2, y: 2, z: 4, core: 2. Of those that a mesh axis runs over, the one named last changes fastest.
Arguments:
- factor: float32 [4, 1024, 4096], P(None, 'row', 'col'), may hold values from -0.125 to 0.125
- panel_inverse: float32 [4, 1024, 1024], P(None, 'row', 'col')
- sim_maps: float32 [4, 1024, 128], P(None, 'row'), may hold values from -6 to 6
- harmonics: bfloat16 [28000, 4096], P('col', 'row'), may hold values from -0.09375 to 0.09375
Outputs:
- solved: float32 [4, 1024, 128], P(None, 'row')
- projected: float32 [128, 28000], P('row', 'col')
The draws below stay inside these ranges and needn't reach their ends.
All inputs are finite; a program needn't handle non-finite values.
Results may differ from the reference program's by a relative error of at most 0.0029.
Values sent between devices are 32-bit elements; how exact they have to be, the bound alone decides.
A program may use at most 64 MiB of HBM per device.

```python
import math
import jax
import jax.numpy as jnp
from jax import lax

P_SIZE = 1024
PANELS = 4
MAPS = 128
MODES = 28000
ROWS = 4096


def draw_panel_inverse(key, part):
    first, second = jax.random.split(jax.random.fold_in(key, 17), 2)
    diagonal = jax.random.uniform(first, (PANELS, P_SIZE), jnp.float32, 1.0, 2.0)
    offdiag = jnp.clip(jax.random.normal(second, (PANELS, P_SIZE, P_SIZE), jnp.float32), -4.0, 4.0) * (0.5 / math.sqrt(P_SIZE))
    unit = jnp.eye(P_SIZE, dtype=jnp.float32)
    matrix = offdiag * (1.0 - unit) + unit * diagonal[:, :, None]
    return matrix


def steps_of(stream_key, extent, pieces, low, top_value):
    def one(axis_at, parts):
        steps = jax.random.uniform(jax.random.fold_in(jax.random.fold_in(stream_key, 6), axis_at), (parts,), jnp.float32, low / len(pieces), top_value / len(pieces))
        return jnp.repeat(jnp.exp(steps), extent[axis_at] // parts).reshape((-1,) + (1,) * (len(extent) - axis_at - 1))

    gain = one(*pieces[0])
    for cut in pieces[1:]:
        gain = gain * one(*cut)
    return gain


def scatter_about(rng, dims, deviation, reach, pieces=(), kind=jnp.bfloat16):
    drawn = jax.random.normal(rng, dims, jnp.float32) * deviation
    if len(pieces) > 0:
        drawn = steps_of(rng, dims, pieces, -0.22, 0.18) * drawn
    return jnp.clip(drawn, min=-reach, max=reach).astype(kind)


def setup_inputs(seed: int = 0) -> dict:
    streams_of = jax.random.split(jax.random.key(seed), 5)
    return {
        "factor": scatter_about(streams_of[0], (PANELS, P_SIZE, P_SIZE * PANELS), (2 * P_SIZE) ** -0.5, 0.125, ((1, 4), (2, 8)), jnp.float32),
        "panel_inverse": draw_panel_inverse(jax.random.fold_in(streams_of[4], 71), 0),
        "sim_maps": scatter_about(streams_of[2], (PANELS, P_SIZE, MAPS), 1.0, 6.0, ((1, 4),), jnp.float32),
        "harmonics": scatter_about(streams_of[3], (MODES, P_SIZE * PANELS), ROWS ** -0.5, 0.09375, ((0, 8), (1, 4))),
    }


def reference(factor, panel_inverse, sim_maps, harmonics):
    blocks = jnp.transpose(factor.reshape(PANELS, P_SIZE, P_SIZE, PANELS), (0, 1, 3, 2))
    solved = jnp.zeros((PANELS, P_SIZE, MAPS), jnp.float32)
    for panel in range(PANELS):
        update = jnp.einsum("ajb,jbm->am", blocks[panel], solved, precision=lax.Precision.HIGHEST)
        rhs_now = sim_maps[panel] - update
        result = jnp.dot(panel_inverse[panel], rhs_now, precision=lax.Precision.HIGHEST, preferred_element_type=jnp.float32)
        solved = solved.at[panel].set(result)
    solved_low = solved.astype(jnp.bfloat16)
    stacked = jnp.transpose(solved_low, (1, 0, 2)).reshape(P_SIZE * PANELS, MAPS)
    coeffs = jnp.dot(harmonics.astype(jnp.float32), stacked.astype(jnp.float32), precision=lax.Precision.HIGHEST, preferred_element_type=jnp.float32)
    return solved, jnp.transpose(coeffs)
```

```python
import functools

import jax
import jax.numpy as jnp
from jax import lax
from jax.experimental import pallas as pl
from jax.experimental.pallas import tpu as pltpu
from jax.sharding import PartitionSpec as P

MESH = pl.DeviceIdType.MESH
CHUNK = 512
LANES = 128
SUBLANES = 8
F32, BF16 = jnp.float32, jnp.bfloat16


def split(value):
    high = value.astype(BF16)
    low = (value - high.astype(F32)).astype(BF16)
    return high, low


def mul(left, right):
    return jnp.dot(left, right, preferred_element_type=F32)


def mul_nt(left, right):
    return lax.dot_general(left, right, (((1,), (1,)), ((), ())), preferred_element_type=F32)


def flip(index, bits):
    step = 1
    while step <= bits:
        if bits & step:
            index = index + (1 - 2 * ((index // step) % 2)) * step
        step *= 2
    return index


def spread_rows(shape, stride, offset):
    row = lax.broadcasted_iota(jnp.int32, shape, 0)
    col = lax.broadcasted_iota(jnp.int32, shape, 1)
    return jnp.where(col == row * stride + offset, 1.0, 0.0).astype(BF16)


def drain(sem, ref):
    pltpu.make_async_copy(ref, ref, sem).wait()


def kernel(
    n_row, n_col, factor_hbm, inv_hbm, sim_hbm, harm_hbm, solved_ref, proj_ref,
    factor, inv, sim, harm, mats, mats_high, mats_low, off_high, off_low, given, turn,
    acts, sol, across, part, landed, place, turned, outs, relayed, final,
    load_sem, ag_send, ag_recv, g_send, g_recv, p_send, p_recv, so_send, so_recv,
    xa_send, xa_recv, rs_send, rs_recv, pj_send, rl_recv, fi_recv,
):
    panels, rows, maps = sim.shape
    cols = inv.shape[2]
    own = maps // n_col
    out_rows = maps // n_row
    stages = 2 * panels - 1
    modes = harm.shape[0]
    chunks = outs.shape[0]
    wide = rows * n_row
    r, c = lax.axis_index("row"), lax.axis_index("col")

    def remote(source, target, send, recv, row, col):
        pltpu.make_async_remote_copy(
            src_ref=source, dst_ref=target, send_sem=send, recv_sem=recv,
            device_id=(row, col), device_id_type=MESH,
        ).start()

    loads = [pltpu.make_async_copy(sim_hbm, sim, load_sem.at[0])]
    loads.append(pltpu.make_async_copy(inv_hbm, inv, load_sem.at[1]))
    for k in range(1, panels):
        loads.append(pltpu.make_async_copy(factor_hbm.at[k], factor.at[k - 1], load_sem.at[1 + k]))
    loads.append(pltpu.make_async_copy(harm_hbm, harm, load_sem.at[1 + panels]))
    for load in loads:
        load.start()

    barrier = pltpu.get_barrier_semaphore()

    def greet_row(d, carry):
        pl.semaphore_signal(
            barrier, inc=1, device_id=((r + d) % n_row, c), device_id_type=MESH
        )
        return carry

    def greet_col(d, carry):
        pl.semaphore_signal(
            barrier, inc=1, device_id=(r, (c + d) % n_col), device_id_type=MESH
        )
        return carry

    lax.fori_loop(1, n_row, greet_row, 0)
    lax.fori_loop(1, n_col, greet_col, 0)

    my_maps = pl.ds(pl.multiple_of(c * own, own), own)
    my_rows = pl.ds(pl.multiple_of(r * rows, rows), rows)
    my_cols = pl.ds(pl.multiple_of(c * cols, cols), cols)

    loads[0].wait()
    for k in range(panels):
        turn[...] = jnp.transpose(sim[k], (1, 0))
        given[k] = turn[my_maps, :]
    acts[0, :, my_rows] = given[0]
    loads[1].wait()
    same = spread_rows((cols, cols), 1, 0)
    for k in range(panels):
        high, low = split(inv[k])
        mats[2 * k, my_cols, :] = mul_nt(same, high) + mul_nt(same, low)
    for k in range(1, panels):
        loads[1 + k].wait()
        high, low = split(factor[k - 1])
        for j in range(k):
            pick = spread_rows((cols, cols * panels), panels, j)
            first, second = mul_nt(pick, high), mul_nt(pick, low)
            if j == k - 1:
                mats[2 * k - 1, my_cols, :] = first + second
            else:
                at = (k - j - 2) * rows
                off_high[j, :, at : at + rows] = first.astype(BF16)
                off_low[j, :, at : at + rows] = second.astype(BF16)
    for k in range(panels):
        place[k] = spread_rows((rows, rows * panels), panels, k)
    pl.semaphore_wait(barrier, n_row + n_col - 2)

    def to_rows(t):
        def one(d, carry):
            remote(acts.at[t, :, my_rows], acts.at[t, :, my_rows],
                   ag_send.at[t], ag_recv.at[t, r], (r + d) % n_row, c)
            return carry

        lax.fori_loop(1, n_row, one, 0)

    def gather(n):
        block = mats.at[n, my_cols]
        for d in range(2, n_col, 2):
            remote(block, block, g_send.at[n], g_recv.at[n, d // 2 - 1], r, flip(c, d))
        remote(block, block, p_send.at[n], p_recv.at[n], r, flip(c, 1))

    def complete(n):
        for d in range(2, n_col, 2):
            block = mats.at[n, pl.ds(pl.multiple_of(flip(c, d) * cols, cols), cols)]
            drain(g_recv.at[n, d // 2 - 1], block)
            remote(block, block, p_send.at[n], p_recv.at[n], r, flip(c, 1))
        drain(p_recv.at[n], mats.at[n, pl.ds(0, n_col // 2 * cols)])
        mats_high[n], mats_low[n] = split(mats[n])

    half = r // (n_row // 2)
    near = r + half * (n_row - 1 - 2 * r)

    def apply(t):
        total = jnp.zeros((2 * own, rows), F32)
        total_low = jnp.zeros((own, rows), F32)
        for i in range(n_row):
            if i == 0:
                source = r
            else:
                source = (i - 1) + jnp.where(i - 1 >= near, 1, 0)
                source = source + half * (n_row - 1 - 2 * source)
            there = pl.ds(pl.multiple_of(source * rows, rows), rows)
            if i > 0:
                drain(ag_recv.at[t, source], acts.at[t, :, there])
            high, low = split(acts[t, :, there])
            both = jnp.concatenate([high, low], axis=0)
            total = total + mul(both, mats_high[t, there, :])
            total_low = total_low + mul(high, mats_low[t, there, :])
        return total[:own] + (total[own:] + total_low)

    def width(j):
        return (panels - 2 - j) * rows

    to_rows(0)
    gather(0)
    gather(1)
    complete(0)
    for t in range(stages):
        value = apply(t)
        if t % 2 == 0:
            k = t // 2
            if t + 1 < stages:
                acts[t + 1, :, my_rows] = value
                to_rows(t + 1)
            sol[k, my_maps, :] = value

            def share(d, carry):
                remote(sol.at[k, my_maps], sol.at[k, my_maps],
                       so_send.at[k], so_recv.at[k], r, (c + d) % n_col)
                return carry

            lax.fori_loop(1, n_col, share, 0)
            j = k - 1
            if 0 <= j < panels - 2:
                drain(xa_recv.at[j], across.at[j, pl.ds(0, (n_col - 1) * own)])
                high, low = split(across[j])
                w = width(j)
                part[j, :, :w] = mul(high, off_high[j, :, :w]) + (
                    mul(high, off_low[j, :, :w]) + mul(low, off_high[j, :, :w])
                )

                def reduce(d, carry):
                    peer = (c + d) % n_col
                    remote(
                        part.at[j, pl.ds(pl.multiple_of(peer * own, own), own), pl.ds(0, w)],
                        landed.at[j, d - 1, :, pl.ds(0, w)],
                        rs_send.at[j], rs_recv.at[j], r, peer,
                    )
                    return carry

                lax.fori_loop(1, n_col, reduce, 0)
        else:
            k = (t + 1) // 2
            for j in range(k - 1):
                at = (k - j - 2) * rows
                if at == 0:
                    drain(rs_recv.at[j], landed.at[j, :, :, pl.ds(0, width(j))])
                value = value + part[j, my_maps, at : at + rows]
                for d in range(n_col - 1):
                    value = value + landed[j, d, :, at : at + rows]
            acts[t + 1, :, my_rows] = given[k] - value
            to_rows(t + 1)
            j = k - 1
            if j < panels - 2:
                def turn_over(d, carry):
                    peer = (c + d) % n_col
                    remote(
                        acts.at[t, :, pl.ds(pl.multiple_of(peer * cols, cols), cols)],
                        across.at[j, my_maps],
                        xa_send.at[j], xa_recv.at[j], r, peer,
                    )
                    return carry

                lax.fori_loop(1, n_col, turn_over, 0)
                across[j, my_maps, :] = acts[t, :, my_cols]
        if t + 2 < stages:
            gather(t + 2)
        if t % 2 == 1:
            k = t // 2
            drain(so_recv.at[k], sol.at[k, pl.ds(0, (n_col - 1) * own)])
            solved_ref[k] = jnp.transpose(sol[k], (1, 0))
            spread = mul(sol[k].astype(BF16), place[k])
            turned[...] = spread if k == 0 else turned[...] + spread
        if t + 1 < stages:
            complete(t + 1)

    loads[-1].wait()
    last = panels - 1
    drain(so_recv.at[last], sol.at[last, pl.ds(0, (n_col - 1) * own)])
    maps_now = (turned[...] + mul(sol[last].astype(BF16), place[last])).astype(BF16)

    partner = flip(r, 1)
    odd = r % 2 == 1

    def slab(s):
        return pl.ds(pl.multiple_of(s * out_rows, out_rows), out_rows)

    def relays(s):
        return (s // 2 != r // 2) & ((s > r) == odd)

    def passes(s):
        return (s // 2 != r // 2) & ((s > r) != odd)

    for i in range(chunks):
        size = min(CHUNK, modes - i * CHUNK)
        outs[i, :, :size] = mul_nt(maps_now, harm[i * CHUNK : i * CHUNK + size, :])
        for s in range(n_row):
            @pl.when(passes(s))
            def _():
                remote(outs.at[i, slab(s)], relayed.at[i, s],
                       pj_send.at[i], rl_recv.at[i, s], partner, c)
    for i in range(chunks):
        remote(outs.at[i, slab(partner)], final.at[i, 0],
               pj_send.at[i], fi_recv.at[i], partner, c)
    solved_ref[last] = jnp.transpose(sol[last], (1, 0))
    for i in range(chunks):
        for s in range(n_row):
            @pl.when(relays(s))
            def _():
                drain(rl_recv.at[i, s], relayed.at[i, s])
                outs[i, slab(s)] = outs[i, slab(s)] + relayed[i, s]
                pair = r // 2
                slot = pair + jnp.where(pair < s // 2, 1, 0)
                remote(outs.at[i, slab(s)], final.at[i, slot],
                       pj_send.at[i], fi_recv.at[i], s, c)
    for i in range(chunks):
        size = min(CHUNK, modes - i * CHUNK)
        drain(fi_recv.at[i], final.at[i])
        value = outs[i, slab(r)]
        for d in range(n_row // 2):
            value = value + final[i, d]
        proj_ref[:, i * CHUNK : i * CHUNK + size] = value[:, :size]

    for t in range(stages):
        drain(ag_send.at[t], acts.at[t, :, pl.ds(0, (n_row - 1) * rows)])
        drain(g_send.at[t], mats.at[t, pl.ds(0, (n_col // 2 - 1) * cols)])
        drain(p_send.at[t], mats.at[t, pl.ds(0, n_col // 2 * cols)])
    for k in range(panels):
        drain(so_send.at[k], sol.at[k, pl.ds(0, (n_col - 1) * own)])
    for j in range(panels - 2):
        drain(xa_send.at[j], across.at[j, pl.ds(0, (n_col - 1) * own)])
        drain(rs_send.at[j], landed.at[j, :, :, pl.ds(0, width(j))])
    for i in range(chunks):
        drain(pj_send.at[i], outs.at[i, pl.ds(0, (n_row - 1) * out_rows)])


def fused(n_row, n_col, factor, inv, sim, harm):
    panels, rows, maps = sim.shape
    cols = inv.shape[2]
    modes = harm.shape[0]
    own = maps // n_col
    wide = rows * n_row
    out_rows = maps // n_row
    stages = 2 * panels - 1
    chunks = -(-modes // CHUNK)
    off_width = (panels - 2) * rows
    any_space = pl.BlockSpec(memory_space=pl.ANY)
    vmem = pl.BlockSpec(memory_space=pltpu.VMEM)
    dma = pltpu.SemaphoreType.DMA
    return pl.pallas_call(
        functools.partial(kernel, n_row, n_col),
        out_shape=(
            jax.ShapeDtypeStruct(sim.shape, F32),
            jax.ShapeDtypeStruct((out_rows, modes), F32),
        ),
        in_specs=[any_space] * 4,
        out_specs=(vmem, vmem),
        scratch_shapes=[
            pltpu.VMEM((panels - 1,) + factor.shape[1:], F32),
            pltpu.VMEM(inv.shape, F32),
            pltpu.VMEM(sim.shape, F32),
            pltpu.VMEM(harm.shape, BF16),
            pltpu.VMEM((stages, wide, rows), F32),
            pltpu.VMEM((stages, wide, rows), BF16),
            pltpu.VMEM((stages, wide, rows), BF16),
            pltpu.VMEM((panels - 2, cols, off_width), BF16),
            pltpu.VMEM((panels - 2, cols, off_width), BF16),
            pltpu.VMEM((panels, own, rows), F32),
            pltpu.VMEM((maps, rows), F32),
            pltpu.VMEM((stages, own, wide), F32),
            pltpu.VMEM((panels, maps, rows), F32),
            pltpu.VMEM((panels - 2, maps, cols), F32),
            pltpu.VMEM((panels - 2, maps, off_width), F32),
            pltpu.VMEM((panels - 2, n_col - 1, own, off_width), F32),
            pltpu.VMEM((panels, rows, rows * panels), BF16),
            pltpu.VMEM((maps, rows * panels), F32),
            pltpu.VMEM((chunks, maps, CHUNK), F32),
            pltpu.VMEM((chunks, n_row, out_rows, CHUNK), F32),
            pltpu.VMEM((chunks, n_row // 2, out_rows, CHUNK), F32),
            dma((panels + 2,)),
            dma((stages,)), dma((stages, n_row)),
            dma((stages,)), dma((stages, n_col // 2 - 1)),
            dma((stages,)), dma((stages,)),
            dma((panels,)), dma((panels,)),
            dma((panels - 2,)), dma((panels - 2,)),
            dma((panels - 2,)), dma((panels - 2,)),
            dma((chunks,)), dma((chunks, n_row)), dma((chunks,)),
        ],
        compiler_params=pltpu.CompilerParams(
            collective_id=0, has_side_effects=True, vmem_limit_bytes=56 * 1024 * 1024
        ),
    )(factor, inv, sim, harm)


def plain(factor, panel_inverse, sim_maps, harmonics):
    panels = factor.shape[0]
    row_count = factor.shape[1]
    col_count = factor.shape[2] // panels
    map_count = sim_maps.shape[2]
    col_index = lax.axis_index("col")
    columns = jnp.zeros((col_count, panels, map_count), jnp.float32)
    results = []
    for panel in range(panels):
        flat_cols = columns.reshape(col_count * panels, map_count)
        partial_value = jnp.dot(
            factor[panel], flat_cols,
            precision=lax.Precision.HIGHEST, preferred_element_type=jnp.float32,
        )
        update = lax.psum(partial_value, "col")
        rhs_now = sim_maps[panel] - update
        whole = lax.all_gather(rhs_now, "row", axis=0, tiled=True)
        piece = lax.dynamic_slice_in_dim(whole, col_index * col_count, col_count, 0)
        partial_inv = jnp.dot(
            panel_inverse[panel], piece,
            precision=lax.Precision.HIGHEST, preferred_element_type=jnp.float32,
        )
        result = lax.psum(partial_inv, "col")
        whole_solved = lax.all_gather(result, "row", axis=0, tiled=True)
        solved_piece = lax.dynamic_slice_in_dim(whole_solved, col_index * col_count, col_count, 0)
        columns = columns.at[:, panel, :].set(solved_piece)
        results.append(result)
    solved = jnp.stack(results)
    solved_low = solved.astype(jnp.bfloat16)
    stacked = jnp.transpose(solved_low, (1, 0, 2)).reshape(row_count * panels, map_count)
    projected = lax.psum_scatter(
        lax.dot_general(
            stacked, harmonics, (((0,), (1,)), ((), ())), preferred_element_type=jnp.float32
        ),
        "row", scatter_dimension=0, tiled=True,
    )
    return (solved, projected)


def solution(mesh):
    n_row, n_col = mesh.shape["row"], mesh.shape["col"]

    def local(factor, panel_inverse, sim_maps, harmonics):
        panels, rows, maps = sim_maps.shape
        cols = panel_inverse.shape[2]
        fits = (
            panels > 2
            and n_row % 2 == 0
            and n_col > 2
            and n_col & (n_col - 1) == 0
            and rows * n_row == cols * n_col
            and rows % LANES == 0
            and cols % LANES == 0
            and maps % LANES == 0
            and maps % (n_col * SUBLANES) == 0
            and maps % (n_row * SUBLANES) == 0
        )
        if not fits:
            return plain(factor, panel_inverse, sim_maps, harmonics)
        return fused(n_row, n_col, factor, panel_inverse, sim_maps, harmonics)

    in_specs = (P(None, "row", "col"), P(None, "row", "col"), P(None, "row", None), P("col", "row"))
    out_specs = (P(None, "row", None), P("row", "col"))
    return jax.shard_map(local, mesh=mesh, in_specs=in_specs, out_specs=out_specs, check_vma=False)
```

```python
import functools

import jax
import jax.numpy as jnp
from jax import lax
from jax.experimental import pallas as pl
from jax.experimental.pallas import tpu as pltpu
from jax.sharding import PartitionSpec as P

MESH = pl.DeviceIdType.MESH
CHUNK = 512
LANES = 128
SUBLANES = 8
F32, BF16 = jnp.float32, jnp.bfloat16


def split(value):
    high = value.astype(BF16)
    low = (value - high.astype(F32)).astype(BF16)
    return high, low


def mul(left, right):
    return jnp.dot(left, right, preferred_element_type=F32)


def mul_nt(left, right):
    return lax.dot_general(left, right, (((1,), (1,)), ((), ())), preferred_element_type=F32)


def flip(index, bits):
    step = 1
    while step <= bits:
        if bits & step:
            index = index + (1 - 2 * ((index // step) % 2)) * step
        step *= 2
    return index


def spread_rows(shape, stride, offset):
    row = lax.broadcasted_iota(jnp.int32, shape, 0)
    col = lax.broadcasted_iota(jnp.int32, shape, 1)
    return jnp.where(col == row * stride + offset, 1.0, 0.0).astype(BF16)


def drain(sem, ref):
    pltpu.make_async_copy(ref, ref, sem).wait()


def kernel(
    n_row, n_col, factor_hbm, inv_hbm, sim_hbm, harm_hbm, solved_ref, proj_ref,
    factor, inv, sim, harm, mats, mats_high, mats_low, off_high, off_low, given, turn,
    acts, sol, across, part, landed, place, turned, outs, relayed, final,
    load_sem, ag_send, ag_recv, g_send, g_recv, d_recv, p_send, p_recv, so_send, so_recv,
    xa_send, xa_recv, rs_send, rs_recv, pj_send, rl_recv, fi_recv,
):
    panels, rows, maps = sim.shape
    cols = inv.shape[2]
    own = maps // n_col
    out_rows = maps // n_row
    stages = 2 * panels - 1
    modes = harm.shape[0]
    chunks = outs.shape[0]
    wide = rows * n_row
    r, c = lax.axis_index("row"), lax.axis_index("col")

    def remote(source, target, send, recv, row, col):
        pltpu.make_async_remote_copy(
            src_ref=source, dst_ref=target, send_sem=send, recv_sem=recv,
            device_id=(row, col), device_id_type=MESH,
        ).start()

    loads = [pltpu.make_async_copy(sim_hbm, sim, load_sem.at[0])]
    loads.append(pltpu.make_async_copy(inv_hbm, inv, load_sem.at[1]))
    for k in range(1, panels):
        loads.append(pltpu.make_async_copy(factor_hbm.at[k], factor.at[k - 1], load_sem.at[1 + k]))
    loads.append(pltpu.make_async_copy(harm_hbm, harm, load_sem.at[1 + panels]))
    for load in loads:
        load.start()

    barrier = pltpu.get_barrier_semaphore()

    def greet_row(d, carry):
        pl.semaphore_signal(
            barrier, inc=1, device_id=((r + d) % n_row, c), device_id_type=MESH
        )
        return carry

    def greet_col(d, carry):
        pl.semaphore_signal(
            barrier, inc=1, device_id=(r, (c + d) % n_col), device_id_type=MESH
        )
        return carry

    lax.fori_loop(1, n_row, greet_row, 0)
    lax.fori_loop(1, n_col, greet_col, 0)

    my_maps = pl.ds(pl.multiple_of(c * own, own), own)
    my_rows = pl.ds(pl.multiple_of(r * rows, rows), rows)
    my_cols = pl.ds(pl.multiple_of(c * cols, cols), cols)

    loads[0].wait()
    for k in range(panels):
        turn[...] = jnp.transpose(sim[k], (1, 0))
        given[k] = turn[my_maps, :]
    acts[0, :, my_rows] = given[0]
    loads[1].wait()
    same = spread_rows((cols, cols), 1, 0)
    for k in range(panels):
        high, low = split(inv[k])
        mats[2 * k, my_cols, :] = mul_nt(same, high) + mul_nt(same, low)
    for k in range(1, panels):
        loads[1 + k].wait()
        high, low = split(factor[k - 1])
        for j in range(k):
            pick = spread_rows((cols, cols * panels), panels, j)
            first, second = mul_nt(pick, high), mul_nt(pick, low)
            if j == k - 1:
                mats[2 * k - 1, my_cols, :] = first + second
            else:
                at = pl.ds(j * cols, cols)
                off_high[k - 2, at, :] = first.astype(BF16)
                off_low[k - 2, at, :] = second.astype(BF16)
    for k in range(panels):
        place[k] = spread_rows((rows, rows * panels), panels, k)
    pl.semaphore_wait(barrier, n_row + n_col - 2)

    def to_rows(t):
        def one(d, carry):
            remote(acts.at[t, :, my_rows], acts.at[t, :, my_rows],
                   ag_send.at[t], ag_recv.at[t, r], (r + d) % n_row, c)
            return carry

        lax.fori_loop(1, n_row, one, 0)

    def piece(n, peer):
        return mats.at[n, pl.ds(pl.multiple_of(peer * cols, cols), cols)]

    def to_partner(n, block):
        remote(block, block, p_send.at[n], p_recv.at[n], r, flip(c, 1))

    def issue(n):
        block = mats.at[n, my_cols]
        for i in range(2):
            remote(block, block, g_send.at[n], g_recv.at[n, i], r, flip(c, 2 + 2 * i))
        if n == 0:
            remote(block, block, g_send.at[n], d_recv.at[n], r, flip(c, 6))
        to_partner(n, block)

    def relay(n):
        for i in range(2):
            peer = flip(c, 2 + 2 * i)
            block = piece(n, peer)
            drain(g_recv.at[n, i], block)
            if n > 0:
                at = peer * cols + i * (cols // 2)
                some = mats.at[n, pl.ds(pl.multiple_of(at, cols // 2), cols // 2)]
                remote(some, some, g_send.at[n], d_recv.at[n], r, flip(c, 4 - 2 * i))
            to_partner(n, block)

    def finish(n):
        block = piece(n, flip(c, 6))
        drain(d_recv.at[n], block)
        to_partner(n, block)

    def land(n):
        drain(p_recv.at[n], mats.at[n, pl.ds(0, n_col // 2 * cols)])
        mats_high[n], mats_low[n] = split(mats[n])

    half = r // (n_row // 2)
    near = r + half * (n_row - 1 - 2 * r)

    def apply(t):
        total = jnp.zeros((2 * own, rows), F32)
        total_low = jnp.zeros((own, rows), F32)
        for i in range(n_row):
            if i == 0:
                source = r
            else:
                source = (i - 1) + jnp.where(i - 1 >= near, 1, 0)
                source = source + half * (n_row - 1 - 2 * source)
            there = pl.ds(pl.multiple_of(source * rows, rows), rows)
            if i > 0:
                drain(ag_recv.at[t, source], acts.at[t, :, there])
            high, low = split(acts[t, :, there])
            both = jnp.concatenate([high, low], axis=0)
            total = total + mul(both, mats_high[t, there, :])
            total_low = total_low + mul(high, mats_low[t, there, :])
        return total[:own] + (total[own:] + total_low)

    def share(k):
        def one(d, carry):
            remote(sol.at[k, my_maps], sol.at[k, my_maps],
                   so_send.at[k], so_recv.at[k], r, (c + d) % n_col)
            return carry

        lax.fori_loop(1, n_col, one, 0)

    to_rows(0)
    for n in range(3):
        issue(n)
    relay(0)
    finish(0)
    land(0)
    for t in range(stages):
        value = apply(t)
        if t % 2 == 0:
            k = t // 2
            if t + 1 < stages:
                acts[t + 1, :, my_rows] = value
                to_rows(t + 1)
            sol[k, my_maps, :] = value

            j = k - 1
            if 0 <= j < panels - 2:
                drain(xa_recv.at[j], across.at[j, pl.ds(0, (n_col - 1) * own)])
                total = jnp.zeros((maps, rows), F32)
                for i in range(j + 1):
                    at = pl.ds(i * cols, cols)
                    high, low = split(across[i])
                    total = total + mul(high, off_high[j, at, :]) + (
                        mul(high, off_low[j, at, :]) + mul(low, off_high[j, at, :])
                    )
                part[j] = total

                def reduce(d, carry):
                    peer = (c + d) % n_col
                    remote(
                        part.at[j, pl.ds(pl.multiple_of(peer * own, own), own)],
                        landed.at[j, d - 1], rs_send.at[j], rs_recv.at[j], r, peer,
                    )
                    return carry

                lax.fori_loop(1, n_col, reduce, 0)
        else:
            k = (t + 1) // 2
            if k > 1:
                drain(rs_recv.at[k - 2], landed.at[k - 2])
                value = value + part[k - 2, my_maps, :]
                for d in range(n_col - 1):
                    value = value + landed[k - 2, d]
            acts[t + 1, :, my_rows] = given[k] - value
            to_rows(t + 1)
            j = k - 1
            if j < panels - 2:
                def turn_over(d, carry):
                    peer = (c + d) % n_col
                    remote(
                        acts.at[t, :, pl.ds(pl.multiple_of(peer * cols, cols), cols)],
                        across.at[j, my_maps],
                        xa_send.at[j], xa_recv.at[j], r, peer,
                    )
                    return carry

                lax.fori_loop(1, n_col, turn_over, 0)
                across[j, my_maps, :] = acts[t, :, my_cols]
        if t == 0:
            relay(1)
        if t + 2 < stages:
            relay(t + 2)
        if t + 3 < stages:
            issue(t + 3)
        if t + 1 < stages:
            finish(t + 1)
        if t == stages - 2:
            for k in range(panels - 1):
                share(k)
        if t == stages - 1:
            share(panels - 1)
        if t + 1 < stages:
            land(t + 1)

    loads[-1].wait()
    last = panels - 1
    for k in range(last):
        drain(so_recv.at[k], sol.at[k, pl.ds(0, (n_col - 1) * own)])
        solved_ref[k] = jnp.transpose(sol[k], (1, 0))
        spread = mul(sol[k].astype(BF16), place[k])
        turned[...] = spread if k == 0 else turned[...] + spread
    drain(so_recv.at[last], sol.at[last, pl.ds(0, (n_col - 1) * own)])
    maps_now = (turned[...] + mul(sol[last].astype(BF16), place[last])).astype(BF16)

    partner = flip(r, 1)
    odd = r % 2 == 1

    def slab(s):
        return pl.ds(pl.multiple_of(s * out_rows, out_rows), out_rows)

    def relays(s):
        return (s // 2 != r // 2) & ((s > r) == odd)

    def passes(s):
        return (s // 2 != r // 2) & ((s > r) != odd)

    for i in range(chunks):
        size = min(CHUNK, modes - i * CHUNK)
        outs[i, :, :size] = mul_nt(maps_now, harm[i * CHUNK : i * CHUNK + size, :])
        for s in range(n_row):
            @pl.when(passes(s))
            def _():
                remote(outs.at[i, slab(s)], relayed.at[i, s],
                       pj_send.at[i], rl_recv.at[i, s], partner, c)
    for i in range(chunks):
        remote(outs.at[i, slab(partner)], final.at[i, 0],
               pj_send.at[i], fi_recv.at[i], partner, c)
    solved_ref[last] = jnp.transpose(sol[last], (1, 0))
    for i in range(chunks):
        for s in range(n_row):
            @pl.when(relays(s))
            def _():
                drain(rl_recv.at[i, s], relayed.at[i, s])
                outs[i, slab(s)] = outs[i, slab(s)] + relayed[i, s]
                pair = r // 2
                slot = pair + jnp.where(pair < s // 2, 1, 0)
                remote(outs.at[i, slab(s)], final.at[i, slot],
                       pj_send.at[i], fi_recv.at[i], s, c)
    for i in range(chunks):
        size = min(CHUNK, modes - i * CHUNK)
        drain(fi_recv.at[i], final.at[i])
        value = outs[i, slab(r)]
        for d in range(n_row // 2):
            value = value + final[i, d]
        proj_ref[:, i * CHUNK : i * CHUNK + size] = value[:, :size]

    for t in range(stages):
        drain(ag_send.at[t], acts.at[t, :, pl.ds(0, (n_row - 1) * rows)])
        drain(g_send.at[t], mats.at[t, pl.ds(0, (n_col // 2 - 1) * cols)])
        drain(p_send.at[t], mats.at[t, pl.ds(0, n_col // 2 * cols)])
    for k in range(panels):
        drain(so_send.at[k], sol.at[k, pl.ds(0, (n_col - 1) * own)])
    for j in range(panels - 2):
        drain(xa_send.at[j], across.at[j, pl.ds(0, (n_col - 1) * own)])
        drain(rs_send.at[j], landed.at[j])
    for i in range(chunks):
        drain(pj_send.at[i], outs.at[i, pl.ds(0, (n_row - 1) * out_rows)])


def fused(n_row, n_col, factor, inv, sim, harm):
    panels, rows, maps = sim.shape
    cols = inv.shape[2]
    modes = harm.shape[0]
    own = maps // n_col
    wide = rows * n_row
    out_rows = maps // n_row
    stages = 2 * panels - 1
    chunks = -(-modes // CHUNK)
    any_space = pl.BlockSpec(memory_space=pltpu.HBM)
    vmem = pl.BlockSpec(memory_space=pltpu.VMEM)
    dma = pltpu.SemaphoreType.DMA
    return pl.pallas_call(
        functools.partial(kernel, n_row, n_col),
        out_shape=(
            jax.ShapeDtypeStruct(sim.shape, F32),
            jax.ShapeDtypeStruct((out_rows, modes), F32),
        ),
        in_specs=[any_space] * 4,
        out_specs=(vmem, vmem),
        scratch_shapes=[
            pltpu.VMEM((panels - 1,) + factor.shape[1:], F32),
            pltpu.VMEM(inv.shape, F32),
            pltpu.VMEM(sim.shape, F32),
            pltpu.VMEM(harm.shape, BF16),
            pltpu.VMEM((stages, wide, rows), F32),
            pltpu.VMEM((stages, wide, rows), BF16),
            pltpu.VMEM((stages, wide, rows), BF16),
            pltpu.VMEM((panels - 2, (panels - 2) * cols, rows), BF16),
            pltpu.VMEM((panels - 2, (panels - 2) * cols, rows), BF16),
            pltpu.VMEM((panels, own, rows), F32),
            pltpu.VMEM((maps, rows), F32),
            pltpu.VMEM((stages, own, wide), F32),
            pltpu.VMEM((panels, maps, rows), F32),
            pltpu.VMEM((panels - 2, maps, cols), F32),
            pltpu.VMEM((panels - 2, maps, rows), F32),
            pltpu.VMEM((panels - 2, n_col - 1, own, rows), F32),
            pltpu.VMEM((panels, rows, rows * panels), BF16),
            pltpu.VMEM((maps, rows * panels), F32),
            pltpu.VMEM((chunks, maps, CHUNK), F32),
            pltpu.VMEM((chunks, n_row, out_rows, CHUNK), F32),
            pltpu.VMEM((chunks, n_row // 2, out_rows, CHUNK), F32),
            dma((panels + 2,)),
            dma((stages,)), dma((stages, n_row)),
            dma((stages,)), dma((stages, 2)), dma((stages,)),
            dma((stages,)), dma((stages,)),
            dma((panels,)), dma((panels,)),
            dma((panels - 2,)), dma((panels - 2,)),
            dma((panels - 2,)), dma((panels - 2,)),
            dma((chunks,)), dma((chunks, n_row)), dma((chunks,)),
        ],
        compiler_params=pltpu.CompilerParams(
            collective_id=0, has_side_effects=True, vmem_limit_bytes=53 * 1024 * 1024
        ),
    )(factor, inv, sim, harm)


def plain(factor, panel_inverse, sim_maps, harmonics):
    panels = factor.shape[0]
    row_count = factor.shape[1]
    col_count = factor.shape[2] // panels
    map_count = sim_maps.shape[2]
    col_index = lax.axis_index("col")
    columns = jnp.zeros((col_count, panels, map_count), jnp.float32)
    results = []
    for panel in range(panels):
        flat_cols = columns.reshape(col_count * panels, map_count)
        partial_value = jnp.dot(
            factor[panel], flat_cols,
            precision=lax.Precision.HIGHEST, preferred_element_type=jnp.float32,
        )
        update = lax.psum(partial_value, "col")
        rhs_now = sim_maps[panel] - update
        whole = lax.all_gather(rhs_now, "row", axis=0, tiled=True)
        piece = lax.dynamic_slice_in_dim(whole, col_index * col_count, col_count, 0)
        partial_inv = jnp.dot(
            panel_inverse[panel], piece,
            precision=lax.Precision.HIGHEST, preferred_element_type=jnp.float32,
        )
        result = lax.psum(partial_inv, "col")
        whole_solved = lax.all_gather(result, "row", axis=0, tiled=True)
        solved_piece = lax.dynamic_slice_in_dim(whole_solved, col_index * col_count, col_count, 0)
        columns = columns.at[:, panel, :].set(solved_piece)
        results.append(result)
    solved = jnp.stack(results)
    solved_low = solved.astype(jnp.bfloat16)
    stacked = jnp.transpose(solved_low, (1, 0, 2)).reshape(row_count * panels, map_count)
    projected = lax.psum_scatter(
        lax.dot_general(
            stacked, harmonics, (((0,), (1,)), ((), ())), preferred_element_type=jnp.float32
        ),
        "row", scatter_dimension=0, tiled=True,
    )
    return (solved, projected)


def solution(mesh):
    n_row, n_col = mesh.shape["row"], mesh.shape["col"]

    def local(factor, panel_inverse, sim_maps, harmonics):
        panels, rows, maps = sim_maps.shape
        cols = panel_inverse.shape[2]
        fits = (
            panels > 2
            and n_row % 2 == 0
            and n_col == 2 ** 3
            and rows * n_row == cols * n_col
            and rows % LANES == 0
            and cols % LANES == 0
            and maps % LANES == 0
            and maps % (n_col * SUBLANES) == 0
            and maps % (n_row * SUBLANES) == 0
        )
        if not fits:
            return plain(factor, panel_inverse, sim_maps, harmonics)
        return fused(n_row, n_col, factor, panel_inverse, sim_maps, harmonics)

    in_specs = (P(None, "row", "col"), P(None, "row", "col"), P(None, "row", None), P("col", "row"))
    out_specs = (P(None, "row", None), P("row", "col"))
    return jax.shard_map(local, mesh=mesh, in_specs=in_specs, out_specs=out_specs, check_vma=False)
```

```python
import functools

import jax
import jax.numpy as jnp
from jax import lax
from jax.experimental import pallas as pl
from jax.experimental.pallas import tpu as pltpu
from jax.sharding import PartitionSpec as P

MESH = pl.DeviceIdType.MESH
CHUNK = 512
LANES = 128
SUBLANES = 8
F32, BF16 = jnp.float32, jnp.bfloat16


def split(value):
    high = value.astype(BF16)
    low = (value - high.astype(F32)).astype(BF16)
    return high, low


def mul(left, right):
    return jnp.dot(left, right, preferred_element_type=F32)


def mul_nt(left, right):
    return lax.dot_general(left, right, (((1,), (1,)), ((), ())), preferred_element_type=F32)


def flip(index, bits):
    step = 1
    while step <= bits:
        if bits & step:
            index = index + (1 - 2 * ((index // step) % 2)) * step
        step *= 2
    return index


def spread_rows(shape, stride, offset):
    row = lax.broadcasted_iota(jnp.int32, shape, 0)
    col = lax.broadcasted_iota(jnp.int32, shape, 1)
    return jnp.where(col == row * stride + offset, 1.0, 0.0).astype(BF16)


def drain(sem, ref):
    pltpu.make_async_copy(ref, ref, sem).wait()


def kernel(
    n_row, n_col, factor_hbm, inv_hbm, sim_hbm, harm_hbm, solved_ref, proj_ref,
    factor, inv, sim, harm, mats, mats_high, mats_low, off_high, off_low, given, turn,
    begin, first, first_high, first_low, first_part, first_landed,
    acts, sol, across, part, landed, place, turned, outs, relayed, final,
    load_sem, fs_send, fs_recv, fr_send, fr_recv, ag_send, ag_recv, g_send, g_recv, d_recv, p_send, p_recv, so_send, so_recv,
    xa_send, xa_recv, rs_send, rs_recv, pj_send, rl_recv, fi_recv,
):
    panels, rows, maps = sim.shape
    cols = inv.shape[2]
    own = maps // n_col
    out_rows = maps // n_row
    stages = 2 * panels - 1
    modes = harm.shape[0]
    chunks = outs.shape[0]
    wide = rows * n_row
    r, c = lax.axis_index("row"), lax.axis_index("col")

    def remote(source, target, send, recv, row, col):
        pltpu.make_async_remote_copy(
            src_ref=source, dst_ref=target, send_sem=send, recv_sem=recv,
            device_id=(row, col), device_id_type=MESH,
        ).start()

    loads = [pltpu.make_async_copy(sim_hbm, sim, load_sem.at[0])]
    loads.append(pltpu.make_async_copy(inv_hbm, inv, load_sem.at[1]))
    for k in range(1, panels):
        loads.append(pltpu.make_async_copy(factor_hbm.at[k], factor.at[k - 1], load_sem.at[1 + k]))
    loads.append(pltpu.make_async_copy(harm_hbm, harm, load_sem.at[1 + panels]))
    for load in loads:
        load.start()

    barrier = pltpu.get_barrier_semaphore()

    def greet_row(d, carry):
        pl.semaphore_signal(
            barrier, inc=1, device_id=((r + d) % n_row, c), device_id_type=MESH
        )
        return carry

    def greet_col(d, carry):
        pl.semaphore_signal(
            barrier, inc=1, device_id=(r, (c + d) % n_col), device_id_type=MESH
        )
        return carry

    pieces = rows // cols
    origin = c // pieces

    def greet_origin(peer, carry):
        pl.semaphore_signal(barrier, inc=1, device_id=(origin, peer), device_id_type=MESH)
        return carry

    lax.fori_loop(1, n_row, greet_row, 0)
    lax.fori_loop(1, n_col, greet_col, 0)

    @pl.when(origin != r)
    def _():
        lax.fori_loop(0, n_col, greet_origin, 0)


    my_maps = pl.ds(pl.multiple_of(c * own, own), own)
    my_rows = pl.ds(pl.multiple_of(r * rows, rows), rows)
    my_cols = pl.ds(pl.multiple_of(c * cols, cols), cols)

    loads[0].wait()
    begin[...] = jnp.transpose(sim[0], (1, 0))
    for k in range(1, panels):
        turn[...] = jnp.transpose(sim[k], (1, 0))
        given[k] = turn[my_maps, :]
    loads[1].wait()
    same = spread_rows((cols, cols), 1, 0)
    for k in range(panels):
        high, low = split(inv[k])
        high, low = mul_nt(same, high), mul_nt(same, low)
        if k == 0:
            first_high[...] = high.astype(BF16)
            first_low[...] = low.astype(BF16)
        else:
            mats[2 * k, my_cols, :] = high + low
    for k in range(1, panels):
        loads[1 + k].wait()
        high, low = split(factor[k - 1])
        for j in range(k):
            pick = spread_rows((cols, cols * panels), panels, j)
            top, rest = mul_nt(pick, high), mul_nt(pick, low)
            if j == k - 1:
                mats[2 * k - 1, my_cols, :] = top + rest
            else:
                at = pl.ds(j * cols, cols)
                off_high[k - 2, at, :] = top.astype(BF16)
                off_low[k - 2, at, :] = rest.astype(BF16)
    for k in range(panels):
        place[k] = spread_rows((rows, rows * panels), panels, k)
    pl.semaphore_wait(barrier, n_row + n_col - 2 + (n_row - 1) * pieces)

    def to_rows(t):
        def one(d, carry):
            remote(acts.at[t, :, my_rows], acts.at[t, :, my_rows],
                   ag_send.at[t], ag_recv.at[t, r], (r + d) % n_row, c)
            return carry

        lax.fori_loop(1, n_row, one, 0)

    def piece(n, peer):
        return mats.at[n, pl.ds(pl.multiple_of(peer * cols, cols), cols)]

    def to_partner(n, block):
        remote(block, block, p_send.at[n], p_recv.at[n], r, flip(c, 1))

    def issue(n):
        block = mats.at[n, my_cols]
        for i in range(2):
            remote(block, block, g_send.at[n], g_recv.at[n, i], r, flip(c, 2 + 2 * i))
        to_partner(n, block)

    def relay(n):
        for i in range(2):
            peer = flip(c, 2 + 2 * i)
            block = piece(n, peer)
            drain(g_recv.at[n, i], block)
            at = peer * cols + i * (cols // 2)
            some = mats.at[n, pl.ds(pl.multiple_of(at, cols // 2), cols // 2)]
            remote(some, some, g_send.at[n], d_recv.at[n], r, flip(c, 4 - 2 * i))
            to_partner(n, block)

    def finish(n):
        block = piece(n, flip(c, 6))
        drain(d_recv.at[n], block)
        to_partner(n, block)

    def land(n):
        drain(p_recv.at[n], mats.at[n, pl.ds(0, n_col // 2 * cols)])
        mats_high[n], mats_low[n] = split(mats[n])

    half = r // (n_row // 2)
    near = r + half * (n_row - 1 - 2 * r)

    def apply(t):
        total = jnp.zeros((2 * own, rows), F32)
        total_low = jnp.zeros((own, rows), F32)
        for i in range(n_row):
            if i == 0:
                source = r
            else:
                source = (i - 1) + jnp.where(i - 1 >= near, 1, 0)
                source = source + half * (n_row - 1 - 2 * source)
            there = pl.ds(pl.multiple_of(source * rows, rows), rows)
            if i > 0:
                drain(ag_recv.at[t, source], acts.at[t, :, there])
            high, low = split(acts[t, :, there])
            both = jnp.concatenate([high, low], axis=0)
            total = total + mul(both, mats_high[t, there, :])
            total_low = total_low + mul(high, mats_low[t, there, :])
        return total[:own] + (total[own:] + total_low)

    def share(k):
        def one(d, carry):
            remote(sol.at[k, my_maps], sol.at[k, my_maps],
                   so_send.at[k], so_recv.at[k], r, (c + d) % n_col)
            return carry

        lax.fori_loop(1, n_col, one, 0)

    def reduce(source, target, send, recv):
        def one(d, carry):
            peer = (c + d) % n_col
            remote(source.at[pl.ds(pl.multiple_of(peer * own, own), own)],
                   target.at[d - 1], send, recv, r, peer)
            return carry

        lax.fori_loop(1, n_col, one, 0)

    def start_out(d, carry):
        for i in range(pieces):
            remote(begin.at[my_maps, pl.ds(i * cols, cols)], first.at[my_maps],
                   fs_send, fs_recv, (r + d) % n_row, r * pieces + i)
        return carry

    lax.fori_loop(1, n_row, start_out, 0)
    issue(1)
    issue(2)

    @pl.when(origin == r)
    def _():
        at = (c % pieces) * cols
        first[...] = begin[:, pl.ds(pl.multiple_of(at, cols), cols)]

    @pl.when(origin != r)
    def _():
        drain(fs_recv, first)

    high, low = split(first[...])
    first_part[...] = mul(high, first_high[...]) + (
        mul(high, first_low[...]) + mul(low, first_high[...])
    )
    reduce(first_part, first_landed, fr_send, fr_recv)
    relay(1)
    issue(3)
    for t in range(stages):
        if t == 0:
            drain(fr_recv, first_landed)
            value = first_part[my_maps, :]
            for d in range(n_col - 1):
                value = value + first_landed[d]
        else:
            value = apply(t)
        if t % 2 == 0:
            k = t // 2
            if t + 1 < stages:
                acts[t + 1, :, my_rows] = value
                to_rows(t + 1)
            sol[k, my_maps, :] = value

            j = k - 1
            if 0 <= j < panels - 2:
                drain(xa_recv.at[j], across.at[j, pl.ds(0, (n_col - 1) * own)])
                total = jnp.zeros((maps, rows), F32)
                for i in range(j + 1):
                    at = pl.ds(i * cols, cols)
                    high, low = split(across[i])
                    total = total + mul(high, off_high[j, at, :]) + (
                        mul(high, off_low[j, at, :]) + mul(low, off_high[j, at, :])
                    )
                part[j] = total

                reduce(part.at[j], landed.at[j], rs_send.at[j], rs_recv.at[j])
        else:
            k = (t + 1) // 2
            if k > 1:
                drain(rs_recv.at[k - 2], landed.at[k - 2])
                value = value + part[k - 2, my_maps, :]
                for d in range(n_col - 1):
                    value = value + landed[k - 2, d]
            acts[t + 1, :, my_rows] = given[k] - value
            to_rows(t + 1)
            j = k - 1
            if j < panels - 2:
                def turn_over(d, carry):
                    peer = (c + d) % n_col
                    remote(
                        acts.at[t, :, pl.ds(pl.multiple_of(peer * cols, cols), cols)],
                        across.at[j, my_maps],
                        xa_send.at[j], xa_recv.at[j], r, peer,
                    )
                    return carry

                lax.fori_loop(1, n_col, turn_over, 0)
                across[j, my_maps, :] = acts[t, :, my_cols]
        if t == stages - 2:
            for k in range(panels - 1):
                share(k)
        if t == stages - 1:
            share(panels - 1)
        if t + 1 < stages:
            finish(t + 1)
        if t + 2 < stages:
            relay(t + 2)
        if t + 4 < stages:
            issue(t + 4)
        if t + 1 < stages:
            land(t + 1)

    loads[-1].wait()
    last = panels - 1
    for k in range(last):
        drain(so_recv.at[k], sol.at[k, pl.ds(0, (n_col - 1) * own)])
        solved_ref[k] = jnp.transpose(sol[k], (1, 0))
        spread = mul(sol[k].astype(BF16), place[k])
        turned[...] = spread if k == 0 else turned[...] + spread
    drain(so_recv.at[last], sol.at[last, pl.ds(0, (n_col - 1) * own)])
    maps_now = (turned[...] + mul(sol[last].astype(BF16), place[last])).astype(BF16)

    partner = flip(r, 1)
    odd = r % 2 == 1

    def slab(s):
        return pl.ds(pl.multiple_of(s * out_rows, out_rows), out_rows)

    def relays(s):
        return (s // 2 != r // 2) & ((s > r) == odd)

    def passes(s):
        return (s // 2 != r // 2) & ((s > r) != odd)

    for i in range(chunks):
        size = min(CHUNK, modes - i * CHUNK)
        outs[i, :, :size] = mul_nt(maps_now, harm[i * CHUNK : i * CHUNK + size, :])
        for s in range(n_row):
            @pl.when(passes(s))
            def _():
                remote(outs.at[i, slab(s)], relayed.at[i, s],
                       pj_send.at[i], rl_recv.at[i, s], partner, c)
    for i in range(chunks):
        remote(outs.at[i, slab(partner)], final.at[i, 0],
               pj_send.at[i], fi_recv.at[i], partner, c)
    solved_ref[last] = jnp.transpose(sol[last], (1, 0))
    for i in range(chunks):
        for s in range(n_row):
            @pl.when(relays(s))
            def _():
                drain(rl_recv.at[i, s], relayed.at[i, s])
                outs[i, slab(s)] = outs[i, slab(s)] + relayed[i, s]
                pair = r // 2
                slot = pair + jnp.where(pair < s // 2, 1, 0)
                remote(outs.at[i, slab(s)], final.at[i, slot],
                       pj_send.at[i], fi_recv.at[i], s, c)
    for i in range(chunks):
        size = min(CHUNK, modes - i * CHUNK)
        drain(fi_recv.at[i], final.at[i])
        value = outs[i, slab(r)]
        for d in range(n_row // 2):
            value = value + final[i, d]
        proj_ref[:, i * CHUNK : i * CHUNK + size] = value[:, :size]

    drain(fs_send, begin.at[pl.ds(0, (n_row - 1) * own)])
    drain(fr_send, first_landed)
    for t in range(1, stages):
        drain(ag_send.at[t], acts.at[t, :, pl.ds(0, (n_row - 1) * rows)])
        drain(g_send.at[t], mats.at[t, pl.ds(0, (n_col // 2 - 1) * cols)])
        drain(p_send.at[t], mats.at[t, pl.ds(0, n_col // 2 * cols)])
    for k in range(panels):
        drain(so_send.at[k], sol.at[k, pl.ds(0, (n_col - 1) * own)])
    for j in range(panels - 2):
        drain(xa_send.at[j], across.at[j, pl.ds(0, (n_col - 1) * own)])
        drain(rs_send.at[j], landed.at[j])
    for i in range(chunks):
        drain(pj_send.at[i], outs.at[i, pl.ds(0, (n_row - 1) * out_rows)])


def fused(n_row, n_col, factor, inv, sim, harm):
    panels, rows, maps = sim.shape
    cols = inv.shape[2]
    modes = harm.shape[0]
    own = maps // n_col
    wide = rows * n_row
    out_rows = maps // n_row
    stages = 2 * panels - 1
    chunks = -(-modes // CHUNK)
    any_space = pl.BlockSpec(memory_space=pltpu.HBM)
    vmem = pl.BlockSpec(memory_space=pltpu.VMEM)
    dma = pltpu.SemaphoreType.DMA
    return pl.pallas_call(
        functools.partial(kernel, n_row, n_col),
        out_shape=(
            jax.ShapeDtypeStruct(sim.shape, F32),
            jax.ShapeDtypeStruct((out_rows, modes), F32),
        ),
        in_specs=[any_space] * 4,
        out_specs=(vmem, vmem),
        scratch_shapes=[
            pltpu.VMEM((panels - 1,) + factor.shape[1:], F32),
            pltpu.VMEM(inv.shape, F32),
            pltpu.VMEM(sim.shape, F32),
            pltpu.VMEM(harm.shape, BF16),
            pltpu.VMEM((stages, wide, rows), F32),
            pltpu.VMEM((stages, wide, rows), BF16),
            pltpu.VMEM((stages, wide, rows), BF16),
            pltpu.VMEM((panels - 2, (panels - 2) * cols, rows), BF16),
            pltpu.VMEM((panels - 2, (panels - 2) * cols, rows), BF16),
            pltpu.VMEM((panels, own, rows), F32),
            pltpu.VMEM((maps, rows), F32),
            pltpu.VMEM((maps, rows), F32),
            pltpu.VMEM((maps, cols), F32),
            pltpu.VMEM((cols, rows), BF16),
            pltpu.VMEM((cols, rows), BF16),
            pltpu.VMEM((maps, rows), F32),
            pltpu.VMEM((n_col - 1, own, rows), F32),
            pltpu.VMEM((stages, own, wide), F32),
            pltpu.VMEM((panels, maps, rows), F32),
            pltpu.VMEM((panels - 2, maps, cols), F32),
            pltpu.VMEM((panels - 2, maps, rows), F32),
            pltpu.VMEM((panels - 2, n_col - 1, own, rows), F32),
            pltpu.VMEM((panels, rows, rows * panels), BF16),
            pltpu.VMEM((maps, rows * panels), F32),
            pltpu.VMEM((chunks, maps, CHUNK), F32),
            pltpu.VMEM((chunks, n_row, out_rows, CHUNK), F32),
            pltpu.VMEM((chunks, n_row // 2, out_rows, CHUNK), F32),
            dma((panels + 2,)),
            dma, dma, dma, dma,
            dma((stages,)), dma((stages, n_row)),
            dma((stages,)), dma((stages, 2)), dma((stages,)),
            dma((stages,)), dma((stages,)),
            dma((panels,)), dma((panels,)),
            dma((panels - 2,)), dma((panels - 2,)),
            dma((panels - 2,)), dma((panels - 2,)),
            dma((chunks,)), dma((chunks, n_row)), dma((chunks,)),
        ],
        compiler_params=pltpu.CompilerParams(
            collective_id=0, has_side_effects=True, vmem_limit_bytes=53 * 1024 * 1024
        ),
    )(factor, inv, sim, harm)


def plain(factor, panel_inverse, sim_maps, harmonics):
    panels = factor.shape[0]
    row_count = factor.shape[1]
    col_count = factor.shape[2] // panels
    map_count = sim_maps.shape[2]
    col_index = lax.axis_index("col")
    columns = jnp.zeros((col_count, panels, map_count), jnp.float32)
    results = []
    for panel in range(panels):
        flat_cols = columns.reshape(col_count * panels, map_count)
        partial_value = jnp.dot(
            factor[panel], flat_cols,
            precision=lax.Precision.HIGHEST, preferred_element_type=jnp.float32,
        )
        update = lax.psum(partial_value, "col")
        rhs_now = sim_maps[panel] - update
        whole = lax.all_gather(rhs_now, "row", axis=0, tiled=True)
        piece = lax.dynamic_slice_in_dim(whole, col_index * col_count, col_count, 0)
        partial_inv = jnp.dot(
            panel_inverse[panel], piece,
            precision=lax.Precision.HIGHEST, preferred_element_type=jnp.float32,
        )
        result = lax.psum(partial_inv, "col")
        whole_solved = lax.all_gather(result, "row", axis=0, tiled=True)
        solved_piece = lax.dynamic_slice_in_dim(whole_solved, col_index * col_count, col_count, 0)
        columns = columns.at[:, panel, :].set(solved_piece)
        results.append(result)
    solved = jnp.stack(results)
    solved_low = solved.astype(jnp.bfloat16)
    stacked = jnp.transpose(solved_low, (1, 0, 2)).reshape(row_count * panels, map_count)
    projected = lax.psum_scatter(
        lax.dot_general(
            stacked, harmonics, (((0,), (1,)), ((), ())), preferred_element_type=jnp.float32
        ),
        "row", scatter_dimension=0, tiled=True,
    )
    return (solved, projected)


def solution(mesh):
    n_row, n_col = mesh.shape["row"], mesh.shape["col"]

    def local(factor, panel_inverse, sim_maps, harmonics):
        panels, rows, maps = sim_maps.shape
        cols = panel_inverse.shape[2]
        fits = (
            panels > 2
            and n_row % 2 == 0
            and n_col == 2 ** 3
            and rows * n_row == cols * n_col
            and rows % cols == 0
            and rows % LANES == 0
            and cols % LANES == 0
            and maps % LANES == 0
            and maps % (n_col * SUBLANES) == 0
            and maps % (n_row * SUBLANES) == 0
        )
        if not fits:
            return plain(factor, panel_inverse, sim_maps, harmonics)
        return fused(n_row, n_col, factor, panel_inverse, sim_maps, harmonics)

    in_specs = (P(None, "row", "col"), P(None, "row", "col"), P(None, "row", None), P("col", "row"))
    out_specs = (P(None, "row", None), P("row", "col"))
    return jax.shard_map(local, mesh=mesh, in_specs=in_specs, out_specs=out_specs, check_vma=False)
```
